32 devices in a mesh: fsdp: 8 (over y, x, core), tp: 4 (over z).
Axes of the slice: x: 2, y: 2, z: 4, core: 2. Of those that a mesh axis runs over, the one named last changes fastest.
Arguments:
- activations: bfloat16 [16384, 768], P(('fsdp', 'tp')), may hold values from -6 to 6
- cotangent: bfloat16 [16384, 768], P(('fsdp', 'tp')), may hold values from -6 to 6
- qkv_weight: float32 [2, 768, 3, 12, 64], P(None, 'fsdp', None, 'tp'), may hold values from -1.2 to 1.2
- out_weight: float32 [2, 12, 64, 768], P(None, 'tp', None, 'fsdp'), may hold values from -0.875 to 0.875
- up_weight: float32 [2, 768, 3072], P(None, 'fsdp', 'tp'), may hold values from -0.21875 to 0.21875
- down_weight: float32 [2, 3072, 768], P(None, 'tp', 'fsdp'), may hold values from -0.109375 to 0.109375
- vector_params: float32 [2, 12, 768], P(None, None, ('fsdp', 'tp')), may hold values from -0.8 to 1.4, as said below
- qkv_first: float32 [2, 768, 3, 12, 64], P(None, 'fsdp', None, 'tp'), may hold values from -112 to 112
- out_first: float32 [2, 12, 64, 768], P(None, 'tp', None, 'fsdp'), may hold values from -112 to 112
- up_first: float32 [2, 768, 3072], P(None, 'fsdp', 'tp'), may hold values from -112 to 112
- down_first: float32 [2, 3072, 768], P(None, 'tp', 'fsdp'), may hold values from -112 to 112
- vector_first: float32 [2, 12, 768], P(None, None, ('fsdp', 'tp')), may hold values from -112 to 112
- qkv_second: float32 [2, 768, 3, 12, 64], P(None, 'fsdp', None, 'tp'), may hold values from 6.5536 to 65.536
- out_second: float32 [2, 12, 64, 768], P(None, 'tp', None, 'fsdp'), may hold values from 6.5536 to 65.536
- up_second: float32 [2, 768, 3072], P(None, 'fsdp', 'tp'), may hold values from 6.5536 to 65.536
- down_second: float32 [2, 3072, 768], P(None, 'tp', 'fsdp'), may hold values from 6.5536 to 65.536
- vector_second: float32 [2, 12, 768], P(None, None, ('fsdp', 'tp')), may hold values from 6.5536 to 65.536
Outputs:
- result: float32 [16384, 768], P(('fsdp', 'tp'))
- input_grad: float32 [16384, 768], P(('fsdp', 'tp'))
- qkv_grad: float32 [2, 768, 3, 12, 64], P(None, 'fsdp', None, 'tp')
- out_grad: float32 [2, 12, 64, 768], P(None, 'tp', None, 'fsdp')
- up_grad: float32 [2, 768, 3072], P(None, 'fsdp', 'tp')
- down_grad: float32 [2, 3072, 768], P(None, 'tp', 'fsdp')
- vector_grad: float32 [2, 12, 768], P(None, None, ('fsdp', 'tp'))
- qkv_new: float32 [2, 768, 3, 12, 64], P(None, 'fsdp', None, 'tp')
- out_new: float32 [2, 12, 64, 768], P(None, 'tp', None, 'fsdp')
- up_new: float32 [2, 768, 3072], P(None, 'fsdp', 'tp')
- down_new: float32 [2, 3072, 768], P(None, 'tp', 'fsdp')
- vector_new: float32 [2, 12, 768], P(None, None, ('fsdp', 'tp'))
- qkv_first_new: float32 [2, 768, 3, 12, 64], P(None, 'fsdp', None, 'tp')
- out_first_new: float32 [2, 12, 64, 768], P(None, 'tp', None, 'fsdp')
- up_first_new: float32 [2, 768, 3072], P(None, 'fsdp', 'tp')
- down_first_new: float32 [2, 3072, 768], P(None, 'tp', 'fsdp')
- vector_first_new: float32 [2, 12, 768], P(None, None, ('fsdp', 'tp'))
- qkv_second_new: float32 [2, 768, 3, 12, 64], P(None, 'fsdp', None, 'tp')
- out_second_new: float32 [2, 12, 64, 768], P(None, 'tp', None, 'fsdp')
- up_second_new: float32 [2, 768, 3072], P(None, 'fsdp', 'tp')
- down_second_new: float32 [2, 3072, 768], P(None, 'tp', 'fsdp')
- vector_second_new: float32 [2, 12, 768], P(None, None, ('fsdp', 'tp'))
The draws below stay inside these ranges and needn't reach their ends.
Inputs may be any that keep to these rules, and one draw needn't show every extreme that they name: `vector_params`: rows 0 and 5 of each layer lie between 0.6 and 1.4.
All inputs are finite; a program needn't handle non-finite values.
Results may differ from the reference program's by a relative error of at most 0.012.
The reference program's roundings to bfloat16 on the way count: a program that leaves them out, or rounds other values in their place, can miss the bound.
Values may be sent and summed in bfloat16 or wider, within the bound.
No kernel may reach another device: no remote copies, remote signals or barrier semaphores. Data moves between devices by JAX's collectives and lax.ppermute only.
A program may use at most 192 MiB of HBM per device.

```python
import math
import jax
import jax.numpy as jnp
from jax import lax

D = 768
HEADS = 12
HEAD_DIM = 64
FF = 3072
FRAMES = 512
LAYERS = 2
STEP = 4
TOKENS = 16384


def draw_qkv_weight(key, part):
    base = jax.random.truncated_normal(key, -4.0, 4.0, (LAYERS, D, 3, HEADS, HEAD_DIM), jnp.float32) * D ** (-0.5)
    return base


def draw_vector_params(key, part):
    base = jax.random.truncated_normal(key, -4.0, 4.0, (LAYERS, 12, D), jnp.float32) * 0.2
    row_number = lax.broadcasted_iota(jnp.int32, (LAYERS, 12, D), 1)
    gain_rows = (row_number == 0) | (row_number == 5)
    return jnp.where(gain_rows, 1.0 + 0.5 * base, base)


def steps_of(own_key, dims, shards, low, high):
    level, own = 1.0, jax.random.fold_in(own_key, 6)
    for position, parts in shards:
        steps = jnp.exp(jax.random.uniform(jax.random.fold_in(own, position), (parts,), jnp.float32, low / len(shards), high / len(shards)))
        level = level * jnp.repeat(steps, dims[position] // parts).reshape([-1 if axis == position else 1 for axis in range(len(dims))])
    return level


def normal_values(stream_key, dims, deviation, most, shards=(), dtype=jnp.bfloat16):
    loudness = steps_of(stream_key, dims, shards, -0.22, 0.18) if shards else 1.0
    drawn = jax.random.normal(stream_key, dims, jnp.float32) * deviation * loudness
    return jnp.minimum(jnp.maximum(drawn, -most), most).astype(dtype)


def setup_inputs(seed: int = 0) -> dict:
    arg_keys = jax.random.split(jax.random.key(seed), 18)
    activations = normal_values(arg_keys[0], (TOKENS, D), 1.0, 6.0, ((0, 32),))
    cotangent = normal_values(arg_keys[1], (TOKENS, D), 1.0, 6.0, ((0, 32),))
    qkv_weight = draw_qkv_weight(jax.random.fold_in(arg_keys[17], 71), 0)
    out_weight = normal_values(arg_keys[3], (LAYERS, HEADS, HEAD_DIM, D), (D // 16) ** -0.5, 0.875, ((1, 4), (3, 8)), jnp.float32)
    up_weight = normal_values(arg_keys[4], (LAYERS, D, FF), D ** -0.5, 0.21875, ((1, 8), (2, 4)), jnp.float32)
    down_weight = normal_values(arg_keys[5], (LAYERS, FF, D), FF ** -0.5, 0.109375, ((1, 4), (2, 8)), jnp.float32)
    vector_params = draw_vector_params(jax.random.fold_in(arg_keys[17], 71), 0)
    qkv_first = normal_values(arg_keys[7], (LAYERS, D, 3, HEADS, HEAD_DIM), (0.15 * TOKENS ** 0.5), 112.0, ((1, 8), (3, 4)), jnp.float32)
    out_first = normal_values(arg_keys[8], (LAYERS, HEADS, HEAD_DIM, D), (0.15 * TOKENS ** 0.5), 112.0, ((1, 4), (3, 8)), jnp.float32)
    up_first = normal_values(arg_keys[9], (LAYERS, D, FF), (0.15 * TOKENS ** 0.5), 112.0, ((1, 8), (2, 4)), jnp.float32)
    down_first = normal_values(arg_keys[10], (LAYERS, FF, D), (0.15 * TOKENS ** 0.5), 112.0, ((1, 4), (2, 8)), jnp.float32)
    vector_first = normal_values(arg_keys[11], (LAYERS, 12, D), (0.15 * TOKENS ** 0.5), 112.0, ((2, 32),), jnp.float32)
    qkv_second = jnp.clip(jnp.exp(math.log(65.536) - 2.3025852 * jax.random.uniform(arg_keys[12], (LAYERS, D, 3, HEADS, HEAD_DIM), jnp.float32) ** steps_of(arg_keys[12], (LAYERS, D, 3, HEADS, HEAD_DIM), ((1, 8), (3, 4)), -0.2, 0.2)), 6.5536, 65.536)
    out_second = jnp.clip(jnp.exp(math.log(65.536) - 2.3025852 * jax.random.uniform(arg_keys[13], (LAYERS, HEADS, HEAD_DIM, D), jnp.float32) ** steps_of(arg_keys[13], (LAYERS, HEADS, HEAD_DIM, D), ((1, 4), (3, 8)), -0.2, 0.2)), 6.5536, 65.536)
    up_second = jnp.clip(jnp.exp(math.log(65.536) - 2.3025852 * jax.random.uniform(arg_keys[14], (LAYERS, D, FF), jnp.float32) ** steps_of(arg_keys[14], (LAYERS, D, FF), ((1, 8), (2, 4)), -0.2, 0.2)), 6.5536, 65.536)
    down_second = jnp.clip(jnp.exp(math.log(65.536) - 2.3025852 * jax.random.uniform(arg_keys[15], (LAYERS, FF, D), jnp.float32) ** steps_of(arg_keys[15], (LAYERS, FF, D), ((1, 4), (2, 8)), -0.2, 0.2)), 6.5536, 65.536)
    vector_second = jnp.clip(jnp.exp(math.log(65.536) - 2.3025852 * jax.random.uniform(arg_keys[16], (LAYERS, 12, D), jnp.float32) ** steps_of(arg_keys[16], (LAYERS, 12, D), ((2, 32),), -0.2, 0.2)), 6.5536, 65.536)
    return dict(activations=activations, cotangent=cotangent, qkv_weight=qkv_weight, out_weight=out_weight, up_weight=up_weight, down_weight=down_weight, vector_params=vector_params, qkv_first=qkv_first, out_first=out_first, up_first=up_first, down_first=down_first, vector_first=vector_first, qkv_second=qkv_second, out_second=out_second, up_second=up_second, down_second=down_second, vector_second=vector_second)


@jax.custom_vjp
def low(v):
    return lax.optimization_barrier(v.astype(jnp.bfloat16)).astype(jnp.float32)

@jax.custom_vjp
def low_back(v):
    return v

def low_keep(v):
    return (low(v), None)

def low_pass(kept, grad):
    return (grad,)

def back_keep(v):
    return (v, None)

def back_low(kept, grad):
    return (low(grad),)
low.defvjp(low_keep, low_pass)
low_back.defvjp(back_keep, back_low)
precise = lax.Precision.HIGHEST
NORM_EPS = 1e-05
ADAM_EPS = 1e-08
BETA_ONE = 0.9
BETA_TWO = 0.999
LEARNING_RATE = 0.02
DECAY_RATE = 0.1
VECTOR_RATE = 0.12
VECTOR_DECAY = 0.0

def round_both(value):
    return low(low_back(value))

def normalize(stream):
    centre = stream - lax.optimization_barrier(jnp.mean(stream, axis=-1, keepdims=True))
    spread = lax.optimization_barrier(jnp.mean(centre * centre, axis=-1, keepdims=True))
    return centre * lax.rsqrt(spread + NORM_EPS)

def attend(pieces):
    queries, keys_all, values = pieces
    scores = low_back(jnp.einsum('qhd,khd->hqk', queries, keys_all, precision=precise)) * HEAD_DIM ** (-0.5)
    attention = jax.nn.softmax(scores, axis=-1)
    return jnp.einsum('hqk,khd->qhd', low(attention), values, precision=precise)

def layer_apply(stream, qkv_layer, out_layer, up_layer, down_layer, vector_rows):
    row_count = stream.shape[0]
    normed = low(normalize(stream) * vector_rows[0] + vector_rows[1])
    projected = jnp.dot(normed, low(qkv_layer).reshape(D, 3 * D), precision=precise)
    queries = round_both(projected[:, :D] + vector_rows[2])
    keys_all = round_both(projected[:, D:2 * D])
    values = round_both(projected[:, 2 * D:] + vector_rows[3])
    clip_shape = (row_count // FRAMES, FRAMES, HEADS, HEAD_DIM)
    attended = lax.map(jax.checkpoint(attend), (queries.reshape(clip_shape), keys_all.reshape(clip_shape), values.reshape(clip_shape)))
    attended = round_both(attended.reshape(row_count, D))
    branch = low_back(jnp.dot(attended, low(out_layer).reshape(D, D), precision=precise)) + vector_rows[4]
    middle = stream + branch
    normed_two = low(normalize(middle) * vector_rows[5] + vector_rows[6])
    preact = low_back(jnp.dot(normed_two, low(up_layer), precision=precise) + vector_rows[8:12].reshape(FF))
    hidden = low(jax.nn.gelu(preact, approximate=False))
    return middle + low_back(jnp.dot(hidden, low(down_layer), precision=precise)) + vector_rows[7]

def forward(params, stream):
    for layer_index in range(LAYERS):
        stream = layer_apply(stream, params[0][layer_index], params[1][layer_index], params[2][layer_index], params[3][layer_index], params[4][layer_index])
    return stream

def adam_update(weight, gradient, moment_one, moment_two, rate, decay):
    one_new = BETA_ONE * moment_one + (1.0 - BETA_ONE) * gradient
    two_new = BETA_TWO * moment_two + (1.0 - BETA_TWO) * gradient * gradient
    corrected_one = one_new / (1.0 - BETA_ONE ** STEP)
    corrected_two = two_new / (1.0 - BETA_TWO ** STEP)
    weight_new = weight - rate * (corrected_one / (jnp.sqrt(corrected_two) + ADAM_EPS) + decay * weight)
    return (weight_new, one_new, two_new)

def reference(activations, cotangent, qkv_weight, out_weight, up_weight, down_weight, vector_params, qkv_first, out_first, up_first, down_first, vector_first, qkv_second, out_second, up_second, down_second, vector_second):
    params = (qkv_weight, out_weight, up_weight, down_weight, vector_params)
    clip_total = TOKENS // FRAMES
    per_group = math.gcd(clip_total, max(1, 4096 // FRAMES))
    group_count = clip_total // per_group
    inputs = activations.astype(jnp.float32).reshape(group_count, per_group * FRAMES, D)
    cotangents = cotangent.astype(jnp.float32).reshape(group_count, per_group * FRAMES, D)

    def accumulate(summed, group_pair):
        group_rows, group_cot = group_pair
        outcome, pullback = jax.vjp(forward, params, group_rows)
        param_grads, row_grads = pullback(group_cot)
        return (jax.tree.map(jnp.add, summed, param_grads), (outcome, row_grads))
    initial = jax.tree.map(jnp.zeros_like, params)
    grads, (outcomes, row_grads) = lax.scan(accumulate, initial, (inputs, cotangents))
    qkv_new, qkv_one, qkv_two = adam_update(qkv_weight, grads[0], qkv_first, qkv_second, LEARNING_RATE, DECAY_RATE)
    out_new, out_one, out_two = adam_update(out_weight, grads[1], out_first, out_second, LEARNING_RATE, DECAY_RATE)
    up_new, up_one, up_two = adam_update(up_weight, grads[2], up_first, up_second, LEARNING_RATE, DECAY_RATE)
    down_new, down_one, down_two = adam_update(down_weight, grads[3], down_first, down_second, LEARNING_RATE, DECAY_RATE)
    vector_new, vector_one, vector_two = adam_update(vector_params, grads[4], vector_first, vector_second, VECTOR_RATE, VECTOR_DECAY)
    return (outcomes.reshape(TOKENS, D), row_grads.reshape(TOKENS, D), grads[0], grads[1], grads[2], grads[3], grads[4], qkv_new, out_new, up_new, down_new, vector_new, qkv_one, out_one, up_one, down_one, vector_one, qkv_two, out_two, up_two, down_two, vector_two)
```

```python
import functools
import math

import jax
import jax.numpy as jnp
from jax import lax
from jax.experimental import pallas as pl
from jax.experimental.pallas import tpu as pltpu
from jax.sharding import PartitionSpec as P

HEAD_DIM = 64
FRAMES = 512
LAYERS = 2
STEP = 4

NORM_EPS = 1e-05
ADAM_EPS = 1e-08
BETA_ONE = 0.9
BETA_TWO = 0.999
LEARNING_RATE = 0.02
DECAY_RATE = 0.1
VECTOR_RATE = 0.12
VECTOR_DECAY = 0.0

BF16 = jnp.bfloat16
F32 = jnp.float32
BOTH = ("fsdp", "tp")


def dot_nn(left, right):
    return lax.dot_general(left, right, (((1,), (0,)), ((), ())), preferred_element_type=F32)


def dot_nt(left, right):
    return lax.dot_general(left, right, (((1,), (1,)), ((), ())), preferred_element_type=F32)


def dot_tn(left, right):
    return lax.dot_general(left, right, (((0,), (0,)), ((), ())), preferred_element_type=F32)


class Layout:
    def __init__(self, fsdp, tp):
        self.fsdp, self.tp = fsdp, tp
        self.square = fsdp == 8
        if self.square:
            self.masks = [dy * 4 + dx * 2 + dc for dc in range(2) for dy in range(2) for dx in range(2)]
        else:
            self.masks = list(range(fsdp))

    def swap(self, value, mask):
        pairs = [
            (f * self.tp + t, (f ^ mask) * self.tp + t)
            for f in range(self.fsdp)
            for t in range(self.tp)
        ]
        return lax.ppermute(value, BOTH, pairs)

    def shift(self, value, step):
        pairs = [
            (f * self.tp + t, f * self.tp + (t + step) % self.tp)
            for f in range(self.fsdp)
            for t in range(self.tp)
        ]
        return lax.ppermute(value, BOTH, pairs)

    def gather(self, shard):
        rows = shard.shape[0]
        column = jnp.stack([shard] + [self.shift(shard, -k) for k in range(1, self.tp)])
        if not self.square:
            blocks = [column]
            bit = 1
            while bit < self.fsdp:
                blocks = blocks + [self.swap(block, bit) for block in blocks]
                bit *= 2
            return [(jnp.concatenate(blocks, axis=1), 0, 0)]
        half = self.tp // 2
        along_x, along_y = self.swap(column, 2), self.swap(column, 4)
        corner_x, corner_y = self.swap(along_x[:half], 4), self.swap(along_y[half:], 2)
        mine = [
            (column, 0, 0),
            (along_x, 0, rows),
            (along_y, 0, 2 * rows),
            (corner_x, 0, 3 * rows),
            (corner_y, half, 3 * rows),
        ]
        return mine + [
            (self.swap(block, 1), start, 4 * rows + first) for block, start, first in mine
        ]

    def scatter(self, low, high):
        tp, rows, columns = self.tp, low.shape[1] // (self.fsdp // 2), low.shape[2]
        dtype = low.dtype

        def add(*terms):
            return functools.reduce(jnp.add, [t.astype(F32) for t in terms]).astype(dtype)

        if self.square:
            half = tp // 2
            own, along_x, along_y, corner_x, corner_y = split_add(low, self.swap(high, 1), half)
            from_x = self.swap(corner_x, 2)
            from_y = self.swap(corner_y, 4)
            along_y = self.swap(part_add(along_y, from_x, 0), 4)
            along_x = self.swap(part_add(along_x, from_y, half), 2)
            pieces = last_add(own, along_x, along_y)
        else:
            whole = jnp.concatenate([low, high], axis=1)
            bit = self.fsdp // 2
            while bit:
                middle = whole.shape[1] // 2
                whole = add(whole[:, :middle], self.swap(whole[:, middle:], bit))
                bit //= 2
            pieces = [whole[k] for k in range(tp)]
        moved = [self.shift(pieces[k], k) for k in range(1, tp)]
        return total_add(pieces[0], *moved)


def call(kernel, name, grid, ins, outs, scratch=(), flops=0, transcendentals=0):
    once = {}
    if grid:
        once = dict(pipeline_mode=pl.Buffered(1))

    def spec(block, index, shape):
        if block is None:
            if not grid:
                return pl.BlockSpec(memory_space=pltpu.VMEM)
            return pl.BlockSpec(shape, lambda *g: (0,) * len(shape), **once)
        return pl.BlockSpec(block, index)

    arrays = [i[0] for i in ins]
    moved = sum(a.size * a.dtype.itemsize for a in arrays)
    moved += sum(math.prod(o[0]) * jnp.dtype(o[1]).itemsize for o in outs)
    extra = dict(grid=grid) if grid else {}
    return pl.pallas_call(
        kernel,
        in_specs=[spec(i[1], i[2] if len(i) > 2 else None, i[0].shape) for i in ins],
        out_specs=[spec(o[2], o[3] if len(o) > 3 else None, o[0]) for o in outs],
        out_shape=[jax.ShapeDtypeStruct(o[0], o[1]) for o in outs],
        scratch_shapes=list(scratch),
        compiler_params=pltpu.CompilerParams(vmem_limit_bytes=56 * 1024 * 1024),
        cost_estimate=pl.CostEstimate(
            flops=int(flops), transcendentals=int(transcendentals), bytes_accessed=int(moved)
        ),
        name=name,
        **extra,
    )(*arrays)


def split_add(low, received, half):
    tp, rows, columns = low.shape[0], low.shape[1] // 4, low.shape[2]
    dtype = low.dtype

    def kernel(a_ref, b_ref, own_ref, x_ref, y_ref, cx_ref, cy_ref):
        step = pl.program_id(0)
        total = (a_ref[0].astype(F32) + b_ref[0].astype(F32)).astype(dtype)
        own_ref[0] = total[:rows]
        x_ref[0] = total[rows : 2 * rows]
        y_ref[0] = total[2 * rows : 3 * rows]

        @pl.when(step < half)
        def _():
            cx_ref[0] = total[3 * rows :]

        @pl.when(step >= half)
        def _():
            cy_ref[0] = total[3 * rows :]

    whole = (1, 4 * rows, columns)
    block = (1, rows, columns)
    ahead = lambda k: (k, 0, 0)
    return call(
        kernel,
        "split_add",
        (tp,),
        [(low, whole, ahead), (received, whole, ahead)],
        [((tp, rows, columns), dtype, block, ahead)] * 3
        + [
            ((half, rows, columns), dtype, block, lambda k: (jnp.minimum(k, half - 1), 0, 0)),
            ((tp - half, rows, columns), dtype, block, lambda k: (jnp.maximum(k - half, 0), 0, 0)),
        ],
    )


def part_add(base, extra, start):
    tp, count = base.shape[0], extra.shape[0]
    block = (1,) + base.shape[1:]

    def kernel(a_ref, b_ref, out_ref):
        step = pl.program_id(0)
        inside = (step >= start) & (step < start + count)

        @pl.when(inside)
        def _():
            out_ref[0] = (a_ref[0].astype(F32) + b_ref[0].astype(F32)).astype(base.dtype)

        @pl.when(jnp.logical_not(inside))
        def _():
            out_ref[0] = a_ref[0]

    return call(
        kernel,
        "part_add",
        (tp,),
        [
            (base, block, lambda k: (k, 0, 0)),
            (extra, block, lambda k: (jnp.clip(k - start, 0, count - 1), 0, 0)),
        ],
        [(base.shape, base.dtype, block, lambda k: (k, 0, 0))],
    )[0]


def last_add(own, first, second):
    tp = own.shape[0]

    def kernel(a_ref, b_ref, c_ref, *out_refs):
        for k in range(tp):
            total = a_ref[k].astype(F32) + b_ref[k].astype(F32) + c_ref[k].astype(F32)
            out_refs[k][...] = total.astype(own.dtype)

    return call(
        kernel,
        "last_add",
        (),
        [(own, None), (first, None), (second, None)],
        [(own.shape[1:], own.dtype, None)] * tp,
    )


def total_add(*terms):
    def kernel(*refs):
        refs[-1][...] = functools.reduce(jnp.add, [r[...].astype(F32) for r in refs[:-1]])

    return call(
        kernel, "total_add", (), [(t, None) for t in terms], [(terms[0].shape, F32, None)]
    )[0]


def split_three(value):
    high = value.astype(BF16)
    rest = value - high.astype(F32)
    middle = rest.astype(BF16)
    return high, middle, (rest - middle.astype(F32)).astype(BF16)


def exact(product, value, selection):
    high, middle, low = split_three(value)
    return product(high, selection) + (product(middle, selection) + product(low, selection))


def selection_of(row, height):
    return (lax.broadcasted_iota(jnp.int32, (height, row.shape[1]), 0) == row).astype(BF16)


def to_own(low, wanted):
    def kernel(x_ref, w_ref, out_ref):
        out_ref[...] = dot_nn(x_ref[...], selection_of(w_ref[...], x_ref.shape[1]))

    return call(
        kernel, "to_own", (), [(low, None), (wanted, None)], [(low.shape, F32, None)],
        flops=2 * low.size * low.shape[1],
    )[0]


def from_own(value, wanted):
    def kernel(x_ref, w_ref, out_ref):
        out_ref[...] = exact(dot_nt, x_ref[...], selection_of(w_ref[...], x_ref.shape[1]))

    return call(
        kernel, "from_own", (), [(value, None), (wanted, None)], [(value.shape, F32, None)],
        flops=6 * value.size * value.shape[1],
    )[0]


def vector_tables(parts, layout, places, width, head_width):
    tp, fsdp = layout.tp, layout.fsdp
    tables = LAYERS * 12
    each = width // (fsdp * tp)
    wanted, source, turned, my_tp = places

    def kernel(*refs):
        part_refs = refs[: len(parts)]
        wanted_ref, source_ref, turned_ref, my_ref, rows_ref, qkv_ref, up_ref, table_ref = refs[
            len(parts) :
        ]
        found = {}
        for ref, (array, start, first) in zip(part_refs, parts):
            for k in range(array.shape[0]):
                for i in range(array.shape[1] // tables):
                    found[first // tables + i, start + k] = ref[k, i * tables : (i + 1) * tables, :]
        mixed = jnp.concatenate(
            [found[p, k] for p in range(fsdp) for k in range(tp)], axis=1
        )
        table = exact(dot_nt, mixed, selection_of(source_ref[...], width))
        table_ref[...] = table
        own = exact(dot_nn, table, selection_of(wanted_ref[...], width))
        heads = exact(dot_nn, table, selection_of(turned_ref[...], width))
        zeros = jnp.zeros((1, head_width), F32)
        for layer in range(LAYERS):
            base = layer * 12
            for row, found_row in enumerate((0, 1, 4, 5, 6, 7)):
                rows_ref[layer, row : row + 1, :] = own[base + found_row : base + found_row + 1]
            for k in range(tp):
                cut = slice(k * head_width, (k + 1) * head_width)
                qkv_ref[layer, k] = jnp.concatenate(
                    [heads[base + 2 : base + 3, cut], zeros, heads[base + 3 : base + 4, cut]], axis=1
                )
                place = base + 8 + lax.rem(my_ref[0] + k, tp)
                up_ref[layer, k] = table_ref[pl.ds(place, 1), :]

    return call_smem(
        kernel,
        "vector_tables",
        [array for array, _, _ in parts] + [wanted, source, turned],
        my_tp,
        [
            ((LAYERS, 6, width), F32),
            ((LAYERS, tp, 1, 3 * head_width), F32),
            ((LAYERS, tp, 1, width), F32),
        ],
        [pltpu.VMEM((tables, width), F32)],
    )


def call_smem(kernel, name, arrays, scalar, outs, scratch):
    return pl.pallas_call(
        kernel,
        in_specs=[pl.BlockSpec(memory_space=pltpu.VMEM)] * len(arrays)
        + [pl.BlockSpec(memory_space=pltpu.SMEM)],
        out_specs=[pl.BlockSpec(memory_space=pltpu.VMEM)] * len(outs),
        out_shape=[jax.ShapeDtypeStruct(s, d) for s, d in outs],
        scratch_shapes=scratch,
        compiler_params=pltpu.CompilerParams(vmem_limit_bytes=32 * 1024 * 1024),
        cost_estimate=pl.CostEstimate(
            flops=0, transcendentals=0, bytes_accessed=sum(a.size * 4 for a in arrays)
        ),
        name=name,
    )(*arrays, scalar)


def vector_payload(sums, layout, places, width, head_width):
    tp, fsdp = layout.tp, layout.fsdp
    tables = LAYERS * 12
    each = width // (fsdp * tp)
    wanted, source, turned, my_tp = places
    arrays = [a for layer in range(LAYERS) for a in sums[layer]]

    def kernel(*refs):
        sum_refs = refs[: len(arrays)]
        wanted_ref, source_ref, turned_ref, my_ref, low_ref, high_ref, table_ref = refs[len(arrays) :]
        to_features = selection_of(wanted_ref[...], width)
        to_heads = selection_of(turned_ref[...], width)
        for layer in range(LAYERS):
            ffn_ref, up_ref, attn_ref, qkv_ref = sum_refs[4 * layer : 4 * layer + 4]
            base = layer * 12
            rows = jnp.concatenate([attn_ref[0:2], ffn_ref[0:4], jnp.zeros((2, width), F32)], axis=0)
            rows = exact(dot_nt, rows, to_features)
            table_ref[base : base + 2] = rows[0:2]
            table_ref[base + 4 : base + 8] = rows[2:6]
            heads = jnp.concatenate(
                [
                    jnp.concatenate(
                        [qkv_ref[k, :, s * head_width : (s + 1) * head_width] for k in range(tp)],
                        axis=1,
                    )
                    for s in (0, 2)
                ]
                + [jnp.zeros((6, width), F32)],
                axis=0,
            )
            table_ref[base + 2 : base + 4] = exact(dot_nt, heads, to_heads)[0:2]
            for k in range(tp):
                table_ref[pl.ds(base + 8 + lax.rem(my_ref[0] + k, tp), 1), :] = up_ref[k]
        mixed = exact(dot_nn, table_ref[...], selection_of(source_ref[...], width))
        for p in range(fsdp):
            ref, place = (low_ref, p) if p < fsdp // 2 else (high_ref, p - fsdp // 2)
            for k in range(tp):
                at = (p * tp + k) * each
                ref[k, place * tables : (place + 1) * tables, :] = mixed[:, at : at + each]

    return call_smem(
        kernel,
        "vector_payload",
        arrays + [wanted, source, turned],
        my_tp,
        [((tp, fsdp // 2 * tables, each), F32)] * 2,
        [pltpu.VMEM((tables, width), F32)],
    )


def normalize(stream):
    centre = stream - jnp.mean(stream, axis=-1, keepdims=True)
    spread = jnp.mean(centre * centre, axis=-1, keepdims=True)
    inverse = lax.rsqrt(spread + NORM_EPS)
    return (centre * inverse, inverse)


def norm_back(grad_normed, normed, inverse):
    centred = grad_normed - jnp.mean(grad_normed, axis=-1, keepdims=True)
    return inverse * (centred - normed * jnp.mean(grad_normed * normed, axis=-1, keepdims=True))


def weight_ins(parts, tp):
    ins = []
    for array, start, _ in parts:
        count = array.shape[0]
        ins.append(
            (
                array,
                (1,) + array.shape[1:],
                lambda j, start=start, count=count: (jnp.clip(j - start, 0, count - 1), 0, 0),
            )
        )
    return ins


def fill(weight_ref, part_refs, parts, tp):
    step = pl.program_id(0)
    for ref, (array, start, first) in zip(part_refs, parts):
        count, rows = array.shape[:2]
        if count == tp:
            weight_ref[first : first + rows, :] = ref[0]
        else:

            @pl.when((step >= start) & (step < start + count))
            def _(ref=ref, first=first, rows=rows):
                weight_ref[first : first + rows, :] = ref[0]


def by_step(shape):
    return (1,) + shape[1:], lambda j: (j,) + (0,) * (len(shape) - 1)


def attn_forward(stream, parts, rows6, qkv_bias, tp):
    tokens, width = stream.shape
    wide = qkv_bias.shape[2]
    head_width = wide // 3
    heads = head_width // HEAD_DIM

    def kernel(*refs):
        stream_ref, rows_ref, bias_ref = refs[:3]
        part_refs = refs[3 : 3 + len(parts)]
        normed_ref, qkv_ref, attended_ref, middle_ref, two_ref, weight_ref = refs[3 + len(parts) :]
        step = pl.program_id(0)

        @pl.when(step == 0)
        def _():
            value = stream_ref[...]
            normed, _ = normalize(value)
            normed_ref[...] = (normed * rows_ref[0:1] + rows_ref[1:2]).astype(BF16)
            middle_ref[...] = value + rows_ref[2:3]

        fill(weight_ref, part_refs, parts, tp)
        qkv_ref[0] = (dot_nn(normed_ref[...], weight_ref[:, :wide]) + bias_ref[0]).astype(BF16)
        pieces = []
        for head in range(heads):
            low = head * HEAD_DIM
            query = qkv_ref[0, :, low : low + HEAD_DIM] * BF16(HEAD_DIM ** (-0.5))
            key = qkv_ref[0, :, head_width + low : head_width + low + HEAD_DIM]
            value = qkv_ref[0, :, 2 * head_width + low : 2 * head_width + low + HEAD_DIM]
            scores = dot_nt(key, query)
            exponent = jnp.exp(scores - jnp.max(scores, axis=0, keepdims=True))
            totals = jnp.sum(exponent, axis=0, keepdims=True)
            pieces.append(dot_tn(value, exponent.astype(BF16)) / totals)
        attended = jnp.concatenate(pieces, axis=0).T.astype(BF16)
        attended_ref[0] = attended
        middle_ref[...] += dot_nt(attended, weight_ref[:, wide:])

        @pl.when(step == tp - 1)
        def _():
            normed, _ = normalize(middle_ref[...])
            two_ref[...] = (normed * rows_ref[3:4] + rows_ref[4:5]).astype(BF16)

    return call(
        kernel,
        "attn_forward",
        (tp,),
        [(stream, None), (rows6, None), (qkv_bias,) + by_step(qkv_bias.shape)]
        + weight_ins(parts, tp),
        [
            ((tokens, width), BF16, None),
            ((tp, tokens, wide), BF16) + by_step((tp, tokens, wide)),
            ((tp, tokens, head_width), BF16) + by_step((tp, tokens, head_width)),
            ((tokens, width), F32, None),
            ((tokens, width), BF16, None),
        ],
        scratch=[pltpu.VMEM((width, wide + head_width), BF16)],
        flops=2 * tp * tokens * width * (wide + head_width) + 8 * tp * heads * tokens**2 * 128,
        transcendentals=tp * heads * tokens**2,
    )


def ffn_forward(middle, two, parts, rows6, up_bias, tp):
    tokens, width = middle.shape
    hidden_width = up_bias.shape[2]

    def kernel(*refs):
        middle_ref, two_in_ref, rows_ref, bias_ref = refs[:4]
        part_refs = refs[4 : 4 + len(parts)]
        out_ref, hidden_ref, slope_ref, weight_ref = refs[4 + len(parts) :]
        step = pl.program_id(0)

        @pl.when(step == 0)
        def _():
            out_ref[...] = middle_ref[...] + rows_ref[5:6]

        fill(weight_ref, part_refs, parts, tp)
        preact = dot_nn(two_in_ref[...], weight_ref[:, :hidden_width]) + bias_ref[0]
        half = 0.5 * (1.0 + lax.erf(preact * 2.0 ** (-0.5)))
        hidden = (preact * half).astype(BF16)
        hidden_ref[0] = hidden
        slope = half + preact * jnp.exp(-0.5 * preact * preact) * (2.0 * math.pi) ** (-0.5)
        slope_ref[0] = slope.astype(BF16)
        out_ref[...] += dot_nt(hidden, weight_ref[:, hidden_width:])

    stored = (tp, tokens, hidden_width)
    return call(
        kernel,
        "ffn_forward",
        (tp,),
        [(middle, None), (two, None), (rows6, None), (up_bias,) + by_step(up_bias.shape)]
        + weight_ins(parts, tp),
        [
            ((tokens, width), F32, None),
            (stored, BF16) + by_step(stored),
            (stored, BF16) + by_step(stored),
        ],
        scratch=[pltpu.VMEM((width, 2 * hidden_width), BF16)],
        flops=4 * tp * tokens * width * hidden_width,
        transcendentals=2 * tp * tokens * hidden_width,
    )


def ffn_backward(grad, middle, two, hidden, slope, parts, rows6, tp):
    tokens, width = middle.shape
    hidden_width = hidden.shape[2]
    half = width // 2

    def kernel(*refs):
        grad_ref, middle_ref, two_in_ref, rows_ref, hidden_ref, slope_ref = refs[:6]
        part_refs = refs[6 : 6 + len(parts)]
        (
            out_ref,
            low_ref,
            high_ref,
            sums_ref,
            up_ref,
            weight_ref,
            branch_ref,
            branch_t_ref,
            two_t_ref,
        ) = refs[6 + len(parts) :]
        step = pl.program_id(0)

        @pl.when(step == 0)
        def _():
            branch = grad_ref[...].astype(BF16)
            branch_ref[...] = branch
            branch_t_ref[...] = branch.T
            two_t_ref[...] = two_in_ref[...].T
            out_ref[...] = jnp.zeros_like(out_ref)

        fill(weight_ref, part_refs, parts, tp)
        grad_hidden = dot_nn(branch_ref[...], weight_ref[:, hidden_width:])
        grad_preact = (grad_hidden * slope_ref[0].astype(F32)).astype(BF16)
        up_ref[0] = jnp.sum(grad_preact.astype(F32), axis=0, keepdims=True)
        out_ref[...] += dot_nt(grad_preact, weight_ref[:, :hidden_width])
        up_grad = dot_nn(two_t_ref[...], grad_preact).astype(BF16)
        low_ref[0, :, :hidden_width] = up_grad[:half]
        high_ref[0, :, :hidden_width] = up_grad[half:]
        down_grad = dot_nn(branch_t_ref[...], hidden_ref[0]).astype(BF16)
        low_ref[0, :, hidden_width:] = down_grad[:half]
        high_ref[0, :, hidden_width:] = down_grad[half:]

        @pl.when(step == tp - 1)
        def _():
            error = out_ref[...]
            normed, inverse = normalize(middle_ref[...])
            upstream = grad_ref[...]
            grad_middle = upstream + norm_back(error * rows_ref[3:4], normed, inverse)
            out_ref[...] = grad_middle
            sums_ref[0:1] = jnp.sum(grad_middle, axis=0, keepdims=True)
            sums_ref[1:2] = jnp.sum(error * normed, axis=0, keepdims=True)
            sums_ref[2:3] = jnp.sum(error, axis=0, keepdims=True)
            sums_ref[3:4] = jnp.sum(upstream, axis=0, keepdims=True)

    gradient = (tp, half, 2 * hidden_width)
    up_shape = (tp, 1, hidden_width)
    return call(
        kernel,
        "ffn_backward",
        (tp,),
        [
            (grad, None),
            (middle, None),
            (two, None),
            (rows6, None),
            (hidden,) + by_step(hidden.shape),
            (slope,) + by_step(slope.shape),
        ]
        + weight_ins(parts, tp),
        [
            ((tokens, width), F32, None),
            (gradient, BF16) + by_step(gradient),
            (gradient, BF16) + by_step(gradient),
            ((4, width), F32, None),
            (up_shape, F32) + by_step(up_shape),
        ],
        scratch=[
            pltpu.VMEM((width, 2 * hidden_width), BF16),
            pltpu.VMEM((tokens, width), BF16),
            pltpu.VMEM((width, tokens), BF16),
            pltpu.VMEM((width, tokens), BF16),
        ],
        flops=8 * tp * tokens * width * hidden_width,
    )


def attn_backward(grad, stream, normed, qkv, attended, parts, rows6, tp):
    tokens, width = stream.shape
    wide = qkv.shape[2]
    head_width = wide // 3
    heads = head_width // HEAD_DIM
    half = width // 2

    def kernel(*refs):
        grad_ref, stream_ref, normed_in_ref, rows_ref, qkv_ref, attended_ref = refs[:6]
        part_refs = refs[6 : 6 + len(parts)]
        (
            out_ref,
            low_ref,
            high_ref,
            sums_ref,
            qkv_sum_ref,
            weight_ref,
            branch_ref,
            branch_t_ref,
            normed_t_ref,
        ) = refs[6 + len(parts) :]
        step = pl.program_id(0)

        @pl.when(step == 0)
        def _():
            branch = grad_ref[...].astype(BF16)
            branch_ref[...] = branch
            branch_t_ref[...] = branch.T
            normed_t_ref[...] = normed_in_ref[...].T
            out_ref[...] = jnp.zeros_like(out_ref)

        fill(weight_ref, part_refs, parts, tp)
        grad_attended = dot_nn(branch_ref[...], weight_ref[:, wide:]).astype(BF16)
        grads = [[], [], []]
        for head in range(heads):
            low = head * HEAD_DIM
            query = qkv_ref[0, :, low : low + HEAD_DIM] * BF16(HEAD_DIM ** (-0.5))
            key = qkv_ref[0, :, head_width + low : head_width + low + HEAD_DIM]
            value = qkv_ref[0, :, 2 * head_width + low : 2 * head_width + low + HEAD_DIM]
            piece = grad_attended[:, low : low + HEAD_DIM]
            scores = dot_nt(key, query)
            exponent = jnp.exp(scores - jnp.max(scores, axis=0, keepdims=True))
            probs = exponent * (1.0 / jnp.sum(exponent, axis=0, keepdims=True))
            product = probs * dot_nt(value, piece)
            grad_scores = (product - probs * jnp.sum(product, axis=0, keepdims=True)).astype(BF16)
            grads[0].append(dot_tn(grad_scores, key) * HEAD_DIM ** (-0.5))
            grads[1].append(dot_nn(grad_scores, query))
            grads[2].append(dot_nn(probs.astype(BF16), piece))
        grad_qkv = jnp.concatenate(grads[0] + grads[1] + grads[2], axis=1).astype(BF16)
        qkv_sum_ref[0] = jnp.sum(grad_qkv.astype(F32), axis=0, keepdims=True)
        out_ref[...] += dot_nt(grad_qkv, weight_ref[:, :wide])
        qkv_grad = dot_nn(normed_t_ref[...], grad_qkv).astype(BF16)
        low_ref[0, :, :wide] = qkv_grad[:half]
        high_ref[0, :, :wide] = qkv_grad[half:]
        out_grad = dot_nn(branch_t_ref[...], attended_ref[0]).astype(BF16)
        low_ref[0, :, wide:] = out_grad[:half]
        high_ref[0, :, wide:] = out_grad[half:]

        @pl.when(step == tp - 1)
        def _():
            error = out_ref[...]
            normed, inverse = normalize(stream_ref[...])
            out_ref[...] = grad_ref[...] + norm_back(error * rows_ref[0:1], normed, inverse)
            sums_ref[0:1] = jnp.sum(error * normed, axis=0, keepdims=True)
            sums_ref[1:2] = jnp.sum(error, axis=0, keepdims=True)

    gradient = (tp, half, wide + head_width)
    qkv_sums = (tp, 1, wide)
    return call(
        kernel,
        "attn_backward",
        (tp,),
        [
            (grad, None),
            (stream, None),
            (normed, None),
            (rows6, None),
            (qkv,) + by_step(qkv.shape),
            (attended,) + by_step(attended.shape),
        ]
        + weight_ins(parts, tp),
        [
            ((tokens, width), F32, None),
            (gradient, BF16) + by_step(gradient),
            (gradient, BF16) + by_step(gradient),
            ((2, width), F32, None),
            (qkv_sums, F32) + by_step(qkv_sums),
        ],
        scratch=[
            pltpu.VMEM((width, wide + head_width), BF16),
            pltpu.VMEM((tokens, width), BF16),
            pltpu.VMEM((width, tokens), BF16),
            pltpu.VMEM((width, tokens), BF16),
        ],
        flops=4 * tp * tokens * width * (wide + head_width) + 20 * tp * heads * tokens**2 * 128,
        transcendentals=tp * heads * tokens**2,
    )


def adam_update(weight, gradient, moment_one, moment_two, rate, decay):
    one_new = BETA_ONE * moment_one + (1.0 - BETA_ONE) * gradient
    two_new = BETA_TWO * moment_two + (1.0 - BETA_TWO) * gradient * gradient
    corrected_one = one_new / (1.0 - BETA_ONE**STEP)
    corrected_two = two_new / (1.0 - BETA_TWO**STEP)
    weight_new = weight - rate * (
        corrected_one / (jnp.sqrt(corrected_two) + ADAM_EPS) + decay * weight
    )
    return (weight_new, one_new, two_new)


def shards_of(qkv, out, up, down):
    rows, wide = qkv.shape
    head_width = wide // 3
    hidden_width = up.shape[1]

    def kernel(qkv_ref, out_in_ref, up_ref, down_ref, attn_ref, ffn_ref):
        attn_ref[:, :wide] = qkv_ref[...].astype(BF16)
        attn_ref[:, wide:] = out_in_ref[...].T.astype(BF16)
        ffn_ref[:, :hidden_width] = up_ref[...].astype(BF16)
        ffn_ref[:, hidden_width:] = down_ref[...].T.astype(BF16)

    return call(
        kernel,
        "shards_of",
        (),
        [(qkv, None), (out, None), (up, None), (down, None)],
        [
            ((rows, wide + head_width), BF16, None),
            ((rows, 2 * hidden_width), BF16, None),
        ],
    )


def body(layout, *args):
    (
        activations,
        cotangent,
        qkv_weight,
        out_weight,
        up_weight,
        down_weight,
        vector_params,
    ) = args[:7]
    firsts, seconds = args[7:12], args[12:17]
    fsdp, tp = layout.fsdp, layout.tp
    width = activations.shape[1]
    rows = width // fsdp
    head_width = qkv_weight.shape[3] * HEAD_DIM
    hidden_width = up_weight.shape[2]
    each = width // (fsdp * tp)
    my_fsdp, my_tp = lax.axis_index("fsdp"), lax.axis_index("tp")
    order = my_fsdp ^ jnp.array(layout.masks, jnp.int32)
    turn = (my_tp + jnp.arange(tp, dtype=jnp.int32)) % tp

    def table(values):
        return values.reshape(1, width).astype(jnp.int32)

    wanted = table(order[:, None] * rows + jnp.arange(rows)[None, :])
    source = table(
        order[:, None, None] * rows
        + turn[None, :, None] * each
        + jnp.arange(each)[None, None, :]
    )
    turned = table(turn[:, None] * head_width + jnp.arange(head_width)[None, :])
    places = (wanted, source, turned, my_tp.reshape(1).astype(jnp.int32))

    attn_parts, ffn_parts = [], []
    for layer in range(LAYERS):
        attn_shard, ffn_shard = shards_of(
            qkv_weight[layer].reshape(rows, 3 * head_width),
            out_weight[layer].reshape(head_width, rows),
            up_weight[layer],
            down_weight[layer],
        )
        if layer == 0:
            vector_parts = layout.gather(vector_params.reshape(LAYERS * 12, each))
        attn_parts.append(layout.gather(attn_shard))
        ffn_parts.append(layout.gather(ffn_shard))
    rows6, qkv_bias, up_bias = vector_tables(vector_parts, layout, places, width, head_width)

    stream = to_own(activations, wanted)
    saved = []
    for layer in range(LAYERS):
        normed, qkv, attended, middle, two = attn_forward(
            stream, attn_parts[layer], rows6[layer], qkv_bias[layer], tp
        )
        output, hidden, slope = ffn_forward(
            middle, two, ffn_parts[layer], rows6[layer], up_bias[layer], tp
        )
        saved.append((stream, normed, qkv, attended, middle, two, hidden, slope))
        stream = output
    result = from_own(stream, wanted)
    grad_stream = to_own(cotangent, wanted)
    attn_grads, ffn_grads, sums = [None] * LAYERS, [None] * LAYERS, [None] * LAYERS
    for layer in reversed(range(LAYERS)):
        stream, normed, qkv, attended, middle, two, hidden, slope = saved[layer]
        grad_stream, low, high, ffn_sums, up_sums = ffn_backward(
            grad_stream, middle, two, hidden, slope, ffn_parts[layer], rows6[layer], tp
        )
        ffn_grads[layer] = layout.scatter(low, high)
        grad_stream, low, high, attn_sums, qkv_sums = attn_backward(
            grad_stream, stream, normed, qkv, attended, attn_parts[layer], rows6[layer], tp
        )
        attn_grads[layer] = layout.scatter(low, high)
        sums[layer] = (ffn_sums, up_sums, attn_sums, qkv_sums)
    vector_halves = vector_payload(sums, layout, places, width, head_width)
    vector_grad = layout.scatter(*vector_halves).reshape(vector_params.shape)
    input_grad = from_own(grad_stream, wanted)

    qkv_grad = jnp.stack([g[:, : 3 * head_width] for g in attn_grads]).reshape(qkv_weight.shape)
    out_grad = jnp.stack([g[:, 3 * head_width :].T for g in attn_grads]).reshape(out_weight.shape)
    up_grad = jnp.stack([g[:, :hidden_width] for g in ffn_grads])
    down_grad = jnp.stack([g[:, hidden_width:].T for g in ffn_grads])
    params = (qkv_weight, out_weight, up_weight, down_weight, vector_params)
    grads = (qkv_grad, out_grad, up_grad, down_grad, vector_grad)
    news = []
    for index in range(5):
        rate, decay = (
            (VECTOR_RATE, VECTOR_DECAY) if index == 4 else (LEARNING_RATE, DECAY_RATE)
        )
        news.append(
            adam_update(params[index], grads[index], firsts[index], seconds[index], rate, decay)
        )
    return (
        (result, input_grad)
        + grads
        + tuple(n[0] for n in news)
        + tuple(n[1] for n in news)
        + tuple(n[2] for n in news)
    )


def solution(mesh):
    layout = Layout(mesh.shape["fsdp"], mesh.shape["tp"])
    parameter_specs = (
        P(None, "fsdp", None, "tp", None),
        P(None, "tp", None, "fsdp"),
        P(None, "fsdp", "tp"),
        P(None, "tp", "fsdp"),
        P(None, None, ("fsdp", "tp")),
    )
    tokens = (P(("fsdp", "tp"), None),) * 2
    return jax.shard_map(
        functools.partial(body, layout),
        mesh=mesh,
        in_specs=tokens + parameter_specs * 3,
        out_specs=tokens + parameter_specs * 4,
        check_vma=False,
    )
```
